32 devices in a mesh: arc: 8 (over z, core), col: 4 (over y, x).
Axes of the slice: x: 2, y: 2, z: 4, core: 2. Of those that a mesh axis runs over, the one named last changes fastest.
Arguments:
- design: bfloat16 [12288, 5120], P('arc', 'col'), may hold values from -0.109375 to 0.109375
- local_design: float32 [16, 12288], P(None, 'arc'), may hold values from -6 to 6
- observed: float32 [12288], P('arc'), may hold values from -6 to 6
- valid_mask: int32 [12288], P('arc'), may hold values 0 or 1
- counts: int32 [64], P('arc'), may hold values from 1 to 192, 7680 in all
Outputs:
- normal: float32 [5120, 5120], P('arc', 'col')
- rhs: float32 [5120], P('col')
The draws below stay inside these ranges and needn't reach their ends.
Inputs may be any that keep to these rules, and one draw needn't show every extreme that they name: Arc a holds counts[a] recorded slots at its start; the rest are padding.
All inputs are finite; a program needn't handle non-finite values. No bound on the sum of `valid_mask` or of `counts` on one device may be relied on, other than what follows from the above.
Results may differ from the reference program's by a relative error of at most 0.0028.
Values may be sent and summed in bfloat16 or wider, within the bound.
A program may use at most 128 MiB of HBM per device.

```python
import math
import jax
import jax.numpy as jnp
import numpy as np
from jax import lax

COEFS = 5120
LOCAL = 16
SLOTS = 192
ARCS_DEV = 8
ARCS = 64
ROWS = 12288


def plant(array, own_key, smallest, largest):
    longest = array.shape.index(max(array.shape))
    spots = []
    for shift in (0, 1):
        where = [jax.random.randint(jax.random.fold_in(own_key, axis), (), 0, length) for axis, length in enumerate(array.shape)]
        where[longest] = (where[longest] + shift) % array.shape[longest]
        spots.append(tuple(where))
    return array.at[spots[0]].set(smallest).at[spots[1]].set(largest)


def with_spikes(array, key, source, target, parts, factor):
    owner, partner = [(jnp.arange(array.shape[dim]) // (array.shape[dim] // parts)).reshape([-1 if axis == dim else 1 for axis in range(array.ndim)]) for dim in (source, target)]
    chosen = jax.random.permutation(key, parts)[partner]
    strong = (owner == chosen) | (owner == (partner + parts // 2) % parts)
    return jnp.where(strong, factor * array, array)


def steps_of(own_key, shape, split, least, top_value):
    level, own = 1.0, jax.random.fold_in(own_key, 6)
    for dim, parts in split:
        steps = jnp.exp(jax.random.uniform(jax.random.fold_in(own, dim), (parts,), jnp.float32, least / len(split), top_value / len(split)))
        level = level * jnp.repeat(steps, shape[dim] // parts).reshape([-1 if axis == dim else 1 for axis in range(len(shape))])
    return level


def split_up(number_of, total, reach, lean):
    weights = [(1 << 20) // math.isqrt(grade ** lean) + 1 for grade in range(2, number_of + 1)]
    surplus, holding = total - reach - (number_of - 1), [1] * (number_of - 1)
    while surplus > 0:
        free = [i for i in range(number_of - 1) if holding[i] < reach]
        whole, left = sum([weights[i] for i in free]), surplus
        for i in free:
            more = min(reach - holding[i], max(1, left * weights[i] // whole), surplus)
            holding[i] = holding[i] + more
            surplus = surplus - more
    return np.array([reach] + holding)


def uneven_parts(stream_key, amount, total, limit, lean):
    if amount == 2:
        one = jax.random.randint(stream_key, (), max(1, total - limit), min(limit, total - 1) + 1)
        return jnp.stack([one, total - one])
    lengths = jnp.asarray(split_up(amount, total, limit, lean), jnp.int32)
    couples = (amount - 1) // 2
    donor, sink = lengths[1:1 + 2 * couples:2], lengths[2:2 + 2 * couples:2]
    slack = jnp.minimum(donor - 1, limit - sink)
    moved = jax.random.randint(jax.random.fold_in(stream_key, 1), (couples,), 0, 1 << 20) % (slack + 1)
    lengths = lengths.at[1:1 + 2 * couples:2].set(donor - moved).at[2:2 + 2 * couples:2].set(sink + moved)
    return lengths[jax.random.permutation(jax.random.fold_in(stream_key, 2), amount)]


def scatter_about(rng, extent, width, reach, cuts=(), kind=jnp.bfloat16):
    gain = steps_of(rng, extent, cuts, -0.22, 0.18) if cuts else 1.0
    values = jax.random.normal(rng, extent, jnp.float32) * width * gain
    return jnp.minimum(jnp.maximum(values, -reach), reach).astype(kind)


def bell_draw_with(stream_key, extent, scale, most, cuts, heavy, kind=jnp.bfloat16):
    values = scale * jax.random.normal(stream_key, extent, jnp.float32)
    if cuts:
        values = values * steps_of(stream_key, extent, cuts, -0.22, 0.18)
    return jnp.clip(with_spikes(values, jax.random.fold_in(stream_key, 3), *heavy), -most, most).astype(kind)


def setup_inputs(seed: int = 0) -> dict:
    key_of = jax.random.split(jax.random.key(seed), 6)
    design = bell_draw_with(key_of[0], (ROWS, COEFS), (ARCS_DEV * SLOTS * 4) ** -0.5, 0.109375, ((0, 8), (1, 4)), (0, 1, 8, 2.0))
    local_design = scatter_about(key_of[1], (LOCAL, ROWS), 1.0, 6.0, ((1, 8),), jnp.float32)
    observed = scatter_about(key_of[2], (ROWS,), 1.0, 6.0, ((0, 8),), jnp.float32)
    valid_mask = plant((jax.random.randint(key_of[3], (ROWS,), 0, 10) < 9).astype(jnp.int32), jax.random.fold_in(key_of[3], 1), 0, 1)
    counts = uneven_parts(key_of[4], ARCS, ARCS * SLOTS * 5 // 8, SLOTS, 2).astype(jnp.int32)
    return dict(design=design, local_design=local_design, observed=observed, valid_mask=valid_mask, counts=counts)


def eliminate(block_design, block_local, block_observed, block_live):
    highest = lax.Precision.HIGHEST
    masked = block_local * block_live[None, :]
    gram_matrix = jnp.dot(masked, block_local.T, precision=highest) + jnp.eye(block_local.shape[0], dtype=jnp.float32)
    factor = jnp.linalg.cholesky(gram_matrix)
    inverse = jax.scipy.linalg.cho_solve((factor, True), jnp.eye(block_local.shape[0], dtype=jnp.float32))
    dense = block_design.astype(jnp.float32)
    cross_terms = jnp.dot(masked, dense, precision=highest)
    cross_obs = jnp.dot(masked, block_observed, precision=highest)
    projector = jnp.dot(inverse, cross_terms, precision=highest)
    projected = block_live[:, None] * (dense - jnp.dot(block_local.T, projector, precision=highest))
    solved_obs = jnp.dot(inverse, cross_obs, precision=highest)
    residual = block_live * (block_observed - jnp.dot(block_local.T, solved_obs, precision=highest))
    return (projected.astype(jnp.bfloat16), residual)

def live_rows(counts, valid_mask):
    slot_count = valid_mask.shape[0] // counts.shape[0]
    inside = jnp.arange(slot_count, dtype=jnp.int32)[None, :] < counts[:, None]
    return inside.reshape(-1).astype(jnp.float32) * valid_mask.astype(jnp.float32)

def reference(design, local_design, observed, valid_mask, counts):
    live_mask = live_rows(counts, valid_mask)
    blocks_design = design.reshape(ARCS, SLOTS, COEFS)
    blocks_local = local_design.reshape(LOCAL, ARCS, SLOTS).transpose(1, 0, 2)
    projected, residual = jax.vmap(eliminate)(blocks_design, blocks_local, observed.reshape(ARCS, SLOTS), live_mask.reshape(ARCS, SLOTS))
    dense = projected.reshape(ROWS, COEFS).astype(jnp.float32)
    normal = jnp.dot(dense.T.astype(jnp.float32), dense.astype(jnp.float32), preferred_element_type=jnp.float32)
    rhs = jnp.dot(residual.reshape(ROWS), dense, precision=lax.Precision.HIGHEST)
    return (normal, rhs)
```

```python
import jax
import jax.numpy as jnp
from jax import lax
from jax.experimental import pallas as pl
from jax.experimental.pallas import tpu as pltpu
from jax.sharding import PartitionSpec as P


def inverse_kernel(gram_ref, out_ref):
    count, size, _ = gram_ref.shape
    row_id = lax.broadcasted_iota(jnp.int32, (count, size, size), 1)
    col_id = lax.broadcasted_iota(jnp.int32, (count, size, size), 2)
    work = gram_ref[...]
    for k in range(size):
        on_row, on_col = row_id == k, col_id == k
        pivot_row = work[:, k : k + 1, :]
        pivot = work[:, k : k + 1, k : k + 1]
        scale = 1.0 / pivot
        column = work[:, :, k : k + 1]
        row = jnp.where(on_col[:, :1, :], scale, pivot_row * scale)
        work = jnp.where(on_row, row, jnp.where(on_col, 0.0, work) - column * row)
    out_ref[...] = work


def inverse_of(gram):
    return pl.pallas_call(
        inverse_kernel, out_shape=jax.ShapeDtypeStruct(gram.shape, jnp.float32)
    )(gram)


def permute(value, route, arcs, cols):
    pairs = []
    for a in range(arcs):
        for c in range(cols):
            target = route(a, c)
            if target is not None:
                pairs.append((a * cols + c, target[0] * cols + target[1]))
    return lax.ppermute(value, ("arc", "col"), pairs)


def project(design, local_design, observed, valid_mask, counts):
    row_count, col_width = design.shape
    arc_count = counts.shape[0]
    slots = row_count // arc_count
    size = local_design.shape[0]
    highest = lax.Precision.HIGHEST
    inside = jnp.arange(slots, dtype=jnp.int32)[None, :] < counts[:, None]
    live = inside.astype(jnp.float32) * valid_mask.reshape(arc_count, slots).astype(jnp.float32)
    local = local_design.reshape(size, arc_count, slots).transpose(1, 0, 2)
    masked = local * live[:, None, :]
    gram = jnp.einsum("aks,als->akl", masked, local, precision=highest) + jnp.eye(size, dtype=jnp.float32)
    inverse = inverse_of(gram)
    solved = jnp.einsum("akl,als->aks", inverse, masked, precision=highest)
    part = jnp.einsum("akt,aks->ats", local, solved, precision=highest)
    weight = live[:, :, None] * (jnp.eye(slots, dtype=jnp.float32) - part)
    top = lax.reduce_precision(weight, 8, 7)
    high, low = top.astype(jnp.bfloat16), (weight - top).astype(jnp.bfloat16)
    blocks = design.reshape(arc_count, slots, col_width)

    def times(piece):
        return jnp.einsum("ats,asc->atc", piece, blocks, preferred_element_type=jnp.float32)

    projected = (times(high) + times(low)).astype(jnp.bfloat16).reshape(row_count, col_width)
    residual = jnp.sum(weight * observed.reshape(arc_count, 1, slots), axis=2).reshape(row_count)
    return projected, residual


def product(left, right):
    return lax.dot_general(left, right, (((0,), (0,)), ((), ())), preferred_element_type=jnp.float32)


def shards(arcs, cols, design, local_design, observed, valid_mask, counts):
    projected, residual = project(design, local_design, observed, valid_mask, counts)
    row_count, col_width = projected.shape
    chips = arcs // 2
    per_chip = chips // cols if chips >= cols else 0
    assert chips == cols and per_chip == 1
    unit = col_width // 2
    arc, col = lax.axis_index("arc"), lax.axis_index("col")
    half, chip = arc % 2, arc // 2

    partner = permute(projected, lambda a, c: (a ^ 1, c), arcs, cols)
    both = (projected, partner)
    mine = jnp.concatenate(
        [lax.dynamic_slice_in_dim(p, half * unit, unit, axis=1) for p in both], axis=0
    )
    first = min(unit, -(-unit // 256) * 128)
    spans = [(0, first), (first, unit)]
    rows2 = 2 * row_count

    held = {0: [[mine[:, lo:hi]] for lo, hi in spans]}
    bits = [1 << k for k in range(cols.bit_length() - 1)]
    order = sorted(range(1, cols), key=lambda s: (bin(s).count("1"), s))
    for s in order:
        held[s] = [None] * len(spans)
    by_level = {}
    for s in order:
        by_level.setdefault(bin(s).count("1"), []).append(s)
    for level in sorted(by_level):
        for p in range(len(spans)):
            for s in by_level[level]:
                via = [b for b in bits if s & b]
                size = rows2 // len(via) // 16 * 16
                edges = [k * size for k in range(len(via))] + [rows2]
                chunks = []
                for k, b in enumerate(via):
                    source = held[s ^ b][p]
                    source = source[0] if len(source) == 1 else jnp.concatenate(source, axis=0)
                    chunks.append(
                        permute(source[edges[k] : edges[k + 1]], lambda a, c, b=b: (a, c ^ b), arcs, cols)
                    )
                held[s][p] = chunks

    def reduced(piece, s, sign):
        def place(a, c):
            return (sign * (a // 2 - (c ^ s))) % chips

        def hop(value, start, stop):
            def route(a, c):
                if place(a, c) != start:
                    return None
                return ((((c ^ s) + sign * stop) % chips) * 2 + a % 2, c)

            return permute(value.astype(jnp.bfloat16), route, arcs, cols).astype(jnp.float32)

        far = chips // 2
        total = piece
        for t in range(far, 1, -1):
            total = total + hop(total, t, t - 1)
        short = piece
        for t in range(far + 1, chips - 1):
            short = short + hop(short, t, t + 1)
        own = jnp.where((col ^ s) == chip, piece, 0.0)
        own = own + hop(total, 1, 0)
        if chips - 1 > 1:
            own = own + hop(short, chips - 1, 0)
        return own

    rhs = jnp.dot(residual, projected.astype(jnp.float32), precision=lax.Precision.HIGHEST)
    step = 1
    while step < arcs:
        rhs = rhs + permute(rhs, lambda a, c, step=step: (a ^ step, c), arcs, cols)
        step *= 2
    held[order[-1]][0], rhs = lax.optimization_barrier((held[order[-1]][0], rhs))

    result = [None] * len(spans)
    for s in [0] + order:
        for p in range(len(spans)):
            piece = None
            offset = 0
            for chunk in held[s][p]:
                stop = offset + chunk.shape[0]
                at = 0
                while offset < stop:
                    which, inner = offset // row_count, offset % row_count
                    take = min(stop - offset, row_count - inner)
                    term = product(chunk[at : at + take], both[which][inner : inner + take])
                    piece = term if piece is None else piece + term
                    offset, at = offset + take, at + take
            part = reduced(piece, s, 1 if p % 2 == 0 else -1)
            result[p] = part if result[p] is None else result[p] + part
    normal = jnp.concatenate(result, axis=0)
    return normal, rhs


def solution(mesh):
    placed = (P("arc", "col"), P(None, "arc"), P("arc"), P("arc"), P("arc"))
    arcs, cols = mesh.shape["arc"], mesh.shape["col"]

    def body(*args):
        return shards(arcs, cols, *args)

    return jax.shard_map(
        body, mesh=mesh, in_specs=placed, out_specs=(P("arc", "col"), P("col")), check_vma=False
    )
```

```python
import jax
import jax.numpy as jnp
from jax import lax
from jax.experimental import pallas as pl
from jax.experimental.pallas import tpu as pltpu
from jax.sharding import PartitionSpec as P


def inverse_kernel(gram_ref, out_ref):
    count, size, _ = gram_ref.shape
    row_id = lax.broadcasted_iota(jnp.int32, (count, size, size), 1)
    col_id = lax.broadcasted_iota(jnp.int32, (count, size, size), 2)
    work = gram_ref[...]
    for k in range(size):
        on_row, on_col = row_id == k, col_id == k
        pivot_row = work[:, k : k + 1, :]
        pivot = work[:, k : k + 1, k : k + 1]
        scale = 1.0 / pivot
        column = work[:, :, k : k + 1]
        row = jnp.where(on_col[:, :1, :], scale, pivot_row * scale)
        work = jnp.where(on_row, row, jnp.where(on_col, 0.0, work) - column * row)
    out_ref[...] = work


def inverse_of(gram):
    return pl.pallas_call(
        inverse_kernel, out_shape=jax.ShapeDtypeStruct(gram.shape, jnp.float32)
    )(gram)


def permute(value, route, arcs, cols):
    pairs = []
    for a in range(arcs):
        for c in range(cols):
            target = route(a, c)
            if target is not None:
                pairs.append((a * cols + c, target[0] * cols + target[1]))
    return lax.ppermute(value, ("arc", "col"), pairs)


def project(design, local_design, observed, valid_mask, counts):
    row_count, col_width = design.shape
    arc_count = counts.shape[0]
    slots = row_count // arc_count
    size = local_design.shape[0]
    highest = lax.Precision.HIGHEST
    inside = jnp.arange(slots, dtype=jnp.int32)[None, :] < counts[:, None]
    live = inside.astype(jnp.float32) * valid_mask.reshape(arc_count, slots).astype(jnp.float32)
    local = local_design.reshape(size, arc_count, slots).transpose(1, 0, 2)
    masked = local * live[:, None, :]
    gram = jnp.einsum("aks,als->akl", masked, local, precision=highest) + jnp.eye(size, dtype=jnp.float32)
    inverse = inverse_of(gram)
    solved = jnp.einsum("akl,als->aks", inverse, masked, precision=highest)
    part = jnp.einsum("akt,aks->ats", local, solved, precision=highest)
    weight = live[:, :, None] * (jnp.eye(slots, dtype=jnp.float32) - part)
    top = lax.reduce_precision(weight, 8, 7)
    high, low = top.astype(jnp.bfloat16), (weight - top).astype(jnp.bfloat16)
    blocks = design.reshape(arc_count, slots, col_width)

    def times(piece):
        return jnp.einsum("ats,asc->atc", piece, blocks, preferred_element_type=jnp.float32)

    projected = (times(high) + times(low)).astype(jnp.bfloat16).reshape(row_count, col_width)
    residual = jnp.sum(weight * observed.reshape(arc_count, 1, slots), axis=2).reshape(row_count)
    return projected, residual


def product(left, right):
    return lax.dot_general(left, right, (((0,), (0,)), ((), ())), preferred_element_type=jnp.float32)


def shards(arcs, cols, design, local_design, observed, valid_mask, counts):
    projected, residual = project(design, local_design, observed, valid_mask, counts)
    row_count, col_width = projected.shape
    chips = arcs // 2
    per_chip = chips // cols if chips >= cols else 0
    assert chips == cols and per_chip == 1
    unit = col_width // 2
    arc, col = lax.axis_index("arc"), lax.axis_index("col")
    half, chip = arc % 2, arc // 2

    partner = permute(projected, lambda a, c: (a ^ 1, c), arcs, cols)
    both = (projected, partner)
    mine = jnp.concatenate(
        [lax.dynamic_slice_in_dim(p, half * unit, unit, axis=1) for p in both], axis=0
    )
    width = 256
    spans = [(lo, min(lo + width, unit)) for lo in range(0, unit, width)]
    rows2 = 2 * row_count

    held = {0: [[mine[:, lo:hi]] for lo, hi in spans]}
    bits = [1 << k for k in range(cols.bit_length() - 1)]
    order = sorted(range(1, cols), key=lambda s: (bin(s).count("1"), s))
    for s in order:
        held[s] = [None] * len(spans)
    by_level = {}
    for s in order:
        by_level.setdefault(bin(s).count("1"), []).append(s)
    for level in sorted(by_level):
        for p in range(len(spans)):
            for s in by_level[level]:
                via = [b for b in bits if s & b]
                size = rows2 // len(via) // 16 * 16
                edges = [k * size for k in range(len(via))] + [rows2]
                chunks = []
                for k, b in enumerate(via):
                    source = held[s ^ b][p]
                    source = source[0] if len(source) == 1 else jnp.concatenate(source, axis=0)
                    chunks.append(
                        permute(source[edges[k] : edges[k + 1]], lambda a, c, b=b: (a, c ^ b), arcs, cols)
                    )
                held[s][p] = chunks

    def reduced(piece, s, sign):
        def place(a, c):
            return (sign * (a // 2 - (c ^ s))) % chips

        def hop(value, start, stop):
            def route(a, c):
                if place(a, c) != start:
                    return None
                return ((((c ^ s) + sign * stop) % chips) * 2 + a % 2, c)

            return permute(value.astype(jnp.bfloat16), route, arcs, cols).astype(jnp.float32)

        far = chips // 2
        total = piece
        for t in range(far, 1, -1):
            total = total + hop(total, t, t - 1)
        short = piece
        for t in range(far + 1, chips - 1):
            short = short + hop(short, t, t + 1)
        own = jnp.where((col ^ s) == chip, piece, 0.0)
        own = own + hop(total, 1, 0)
        if chips - 1 > 1:
            own = own + hop(short, chips - 1, 0)
        return own

    rhs = jnp.dot(residual, projected.astype(jnp.float32), precision=lax.Precision.HIGHEST)
    step = 1
    while step < arcs:
        rhs = rhs + permute(rhs, lambda a, c, step=step: (a ^ step, c), arcs, cols)
        step *= 2
    held[order[-1]][0], rhs = lax.optimization_barrier((held[order[-1]][0], rhs))

    result = [None] * len(spans)
    for s in [0] + order:
        for p in range(len(spans)):
            piece = None
            offset = 0
            for chunk in held[s][p]:
                stop = offset + chunk.shape[0]
                at = 0
                while offset < stop:
                    which, inner = offset // row_count, offset % row_count
                    take = min(stop - offset, row_count - inner)
                    term = product(chunk[at : at + take], both[which][inner : inner + take])
                    piece = term if piece is None else piece + term
                    offset, at = offset + take, at + take
            part = reduced(piece, s, 1 if p % 2 == 0 else -1)
            result[p] = part if result[p] is None else result[p] + part
    normal = jnp.concatenate(result, axis=0)
    return normal, rhs


def solution(mesh):
    placed = (P("arc", "col"), P(None, "arc"), P("arc"), P("arc"), P("arc"))
    arcs, cols = mesh.shape["arc"], mesh.shape["col"]

    def body(*args):
        return shards(arcs, cols, *args)

    return jax.shard_map(
        body, mesh=mesh, in_specs=placed, out_specs=(P("arc", "col"), P("col")), check_vma=False
    )
```
